32 devices in a mesh: ctx: 8 (over z, y), head: 4 (over x, core).
Axes of the slice: x: 2, y: 2, z: 4, core: 2. Of those that a mesh axis runs over, the one named last changes fastest.
Arguments:
- queries: bfloat16 [8192, 1024], P('ctx', 'head'), parts along dimension 1, may hold values from -15 to 15
- key_rows: bfloat16 [8192, 512], P('ctx', 'head'), parts along dimension 1, may hold values from -6 to 6
- value_rows: bfloat16 [8192, 512], P('ctx', 'head'), parts along dimension 1, may hold values from -16 to 16
- block_order: int32 [8], replicated, may hold values from 0 to 7, each once
Outputs:
- attended: bfloat16 [8192, 1024], P('ctx', 'head'), parts along dimension 1
The draws below stay inside these ranges and needn't reach their ends.
There are 4 independent parts, one for each index of `head`. The reference program is written for one: setup_inputs(seed, part) draws one part's arguments, and reference() takes and returns one part's arrays. A program takes and returns all parts, laid end to end along the dimension named above; an argument that names none is the same for every part. Nothing has to cross between parts.
Inputs may be any that keep to these rules, and one draw needn't show every extreme that they name: `block_order`: each block number appears once.
All inputs are finite; a program needn't handle non-finite values.
Results may differ from the reference program's by a relative error of at most 0.0033.
Values may be sent and summed in bfloat16 or wider, within the bound.
A program may use at most 128 MiB of HBM per device.

```python
import jax
import jax.numpy as jnp
from jax import lax

HD = 128
QH = 2
TOK_DEV = 1024
BLOCKS = 8
SEQ = 8192


def paired_rows(key):
    folded = jax.random.fold_in(key, 2711)
    query_key, row_key = jax.random.split(folded, 2)
    queries = jnp.clip(2.5 * jax.random.normal(query_key, (SEQ, QH * HD), jnp.float32), -15.0, 15.0)
    key_rows = jnp.clip(jax.random.normal(row_key, (SEQ, HD), jnp.float32), -6.0, 6.0)
    return (queries, key_rows)


def draw_queries(key, part):
    return paired_rows(key)[0].astype(jnp.bfloat16)


def draw_key_rows(key, part):
    return paired_rows(key)[1].astype(jnp.bfloat16)


def block_levels(rng, dims, cuts, low, top_value):
    level = 1.0
    for position, blocks in cuts:
        heights = jax.random.uniform(jax.random.fold_in(jax.random.fold_in(rng, 6), position), (blocks,), jnp.float32, low / len(cuts), top_value / len(cuts))
        level = level * jnp.repeat(jnp.exp(heights), dims[position] // blocks).reshape((-1,) + (1,) * (len(dims) - 1 - position))
    return level


def bell_draw(own_key, dims, deviation, bound, cuts=(), kind=jnp.bfloat16):
    level = block_levels(own_key, dims, cuts, -0.22, 0.18) if cuts else 1.0
    entries = jax.random.normal(own_key, dims, jnp.float32) * deviation * level
    return jnp.minimum(jnp.maximum(entries, -bound), bound).astype(kind)


def setup_inputs(seed: int = 0, part: int = 0) -> dict:
    key_list = jax.random.split(jax.random.key(seed), 5)
    part_splits = jax.random.split(jax.random.fold_in(key_list[4], part), 5)
    queries = draw_queries(jax.random.fold_in(jax.random.fold_in(key_list[4], part), 71), part)
    key_rows = draw_key_rows(jax.random.fold_in(jax.random.fold_in(key_list[4], part), 71), part)
    value_rows = bell_draw(part_splits[2], (SEQ, HD), 4.0, 16.0, ((0, 8),))
    block_order = jax.random.permutation(key_list[3], BLOCKS).astype(jnp.int32)
    return dict(queries=queries, key_rows=key_rows, value_rows=value_rows, block_order=block_order)


score_scale = 168.0 ** -0.5


def positions_of(block_order, count):
    row_ids = jnp.arange(count, dtype=jnp.int32)
    return block_order[row_ids // TOK_DEV] * TOK_DEV + row_ids % TOK_DEV


def reference(queries, key_rows, value_rows, block_order):
    key_pos = positions_of(block_order, SEQ)
    keys_wide = key_rows.astype(jnp.float32)
    values_wide = value_rows.astype(jnp.float32)

    def one_block(block_index):
        row_start = block_index * TOK_DEV
        query_block = lax.dynamic_slice_in_dim(queries, row_start, TOK_DEV, 0)
        query_block = query_block.astype(jnp.float32).reshape(TOK_DEV, QH, HD)
        query_pos = lax.dynamic_slice_in_dim(key_pos, row_start, TOK_DEV, 0)

        def key_step(carry, key_index):
            run_sum, run_max, run_total = carry
            key_start = key_index * TOK_DEV
            tile_keys = lax.dynamic_slice_in_dim(keys_wide, key_start, TOK_DEV, 0)
            tile_values = lax.dynamic_slice_in_dim(values_wide, key_start, TOK_DEV, 0)
            tile_pos = lax.dynamic_slice_in_dim(key_pos, key_start, TOK_DEV, 0)
            scores = jnp.einsum("qhd,kd->hqk", query_block, tile_keys) * score_scale
            visible = tile_pos[None, :] <= query_pos[:, None]
            scores = jnp.where(visible[None], scores, -jnp.inf)
            block_max = jnp.maximum(jnp.max(scores, axis=2), -1e30)
            weights = jnp.exp(scores - block_max[:, :, None])
            block_total = jnp.sum(weights, axis=2)
            rounded = lax.optimization_barrier(weights.astype(jnp.bfloat16)).astype(jnp.float32)
            block_sum = jnp.einsum("hqk,kd->hqd", rounded, tile_values)
            new_max = jnp.maximum(run_max, block_max)
            scale_old = jnp.exp(run_max - new_max)
            scale_new = jnp.exp(block_max - new_max)
            run_sum = run_sum * scale_old[:, :, None] + block_sum * scale_new[:, :, None]
            run_total = run_total * scale_old + block_total * scale_new
            return (run_sum, new_max, run_total), None

        start = (jnp.zeros((QH, TOK_DEV, HD), jnp.float32),
                 jnp.full((QH, TOK_DEV), -1e30, jnp.float32),
                 jnp.zeros((QH, TOK_DEV), jnp.float32))
        final, unused = lax.scan(key_step, start, jnp.arange(BLOCKS, dtype=jnp.int32))
        blended = final[0] / final[2][:, :, None]
        return blended.transpose(1, 0, 2).reshape(TOK_DEV, QH * HD).astype(jnp.bfloat16)

    outputs = lax.map(one_block, jnp.arange(BLOCKS, dtype=jnp.int32))
    return outputs.reshape(SEQ, QH * HD)
```

```python
import functools

import jax
import jax.numpy as jnp
from jax import lax
from jax.experimental import pallas as pl
from jax.experimental.pallas import tpu as pltpu
from jax.sharding import PartitionSpec as P

HD = 128
QH = 2
PARTS = 4
TILES = 4
SCALE2 = 168.0 ** (-0.5) * 1.4426950408889634
LOW = -1e30


def ring_place(index, count):
    side = lax.rem(index, 2)
    level = lax.div(index, 2)
    return level * (1 - side) + (count - 1 - level) * side


def ring_index(place, count):
    side = lax.div(place, count // 2)
    level = place * (1 - side) + (count - 1 - place) * side
    return level * 2 + side


def lanes(column, width):
    return jnp.concatenate([column] * (width // HD), axis=1)


def dot_t(a, b):
    return lax.dot_general(a, b, (((1,), (1,)), ((), ())), preferred_element_type=jnp.float32)


def lane_sum(weights):
    total = weights[:, :HD]
    for start in range(HD, weights.shape[1], HD):
        total = total + weights[:, start : start + HD]
    return total


def kernel(
    count, order_hbm, q_hbm, k_hbm, v_hbm, out_ref,
    order_ref, q_ref, kv_ref, from_left, from_right, tail_keys, tail_values, tail_weights, acc, peak, total,
    to_right_sem, to_left_sem, from_left_sem, from_right_sem, loaded,
):
    me = lax.axis_index("ctx")
    rows = q_ref.shape[0]
    piece = rows // PARTS
    whole = count // 2 - 1
    steps = PARTS * whole
    tails = PARTS // 2
    place = ring_place(me, count)
    right = ring_index(lax.rem(place + 1, count), count)
    left = ring_index(lax.rem(place + count - 1, count), count)

    barrier = pltpu.get_barrier_semaphore()
    for neighbour in (left, right):
        pl.semaphore_signal(barrier, inc=1, device_id={"ctx": neighbour}, device_id_type=pl.DeviceIdType.MESH)
    moves = [(k_hbm, kv_ref.at[0]), (v_hbm, kv_ref.at[1]), (q_hbm, q_ref), (order_hbm, order_ref)]
    loads = [pltpu.make_async_copy(src, dst, loaded.at[i]) for i, (src, dst) in enumerate(moves)]
    for load in loads:
        load.start()
    for load in loads[:2]:
        load.wait()
    pl.semaphore_wait(barrier, 2)

    def remote(src, dst, j, rightward):
        send, recv, target = (to_right_sem, from_left_sem, right) if rightward else (to_left_sem, from_right_sem, left)
        return pltpu.make_async_remote_copy(
            src_ref=src, dst_ref=dst, send_sem=send.at[j], recv_sem=recv.at[j],
            device_id={"ctx": target}, device_id_type=pl.DeviceIdType.MESH,
        )

    def side(j, rightward):
        part = lax.rem(j + (0 if rightward else tails), PARTS)
        return pl.ds(pl.multiple_of(part * piece, piece), piece)

    def landing(j, rightward):
        return (from_left if rightward else from_right).at[lax.div(j, PARTS), :, side(j, rightward)]

    def forward(j, rightward):
        return remote(landing(j - PARTS, rightward), landing(j, rightward), j, rightward)

    def tail_copy(i, which, rightward):
        src, own = (from_left, 0) if rightward else (from_right, 1)
        dst = (tail_keys, tail_values)[which]
        return remote(
            src.at[whole - 1, which, side(i, rightward)], dst.at[i, own], steps + 2 * i + which, rightward
        )

    for j in range(PARTS):
        for rightward in (True, False):
            remote(kv_ref.at[:, side(j, rightward)], landing(j, rightward), j, rightward).start()
    for load in loads[2:]:
        load.wait()

    tile_rows = rows // TILES
    for head in range(QH):
        cols = slice(head * HD, (head + 1) * HD)
        for tile in range(TILES):
            here = slice(tile * tile_rows, (tile + 1) * tile_rows)
            width = (tile + 1) * tile_rows
            scores = dot_t(q_ref[here, cols], kv_ref[0, :width])
            row_ids = lax.broadcasted_iota(jnp.int32, (tile_rows, width), 0) + tile * tile_rows
            column_ids = lax.broadcasted_iota(jnp.int32, (tile_rows, width), 1)
            scores = jnp.where(column_ids <= row_ids, scores, LOW)
            top = jnp.broadcast_to(jnp.max(scores, axis=1, keepdims=True), (tile_rows, HD))
            weights = jnp.exp2((scores - lanes(top, width)) * SCALE2)
            total[head, here, :] = lane_sum(weights)
            acc[head, here, :] = jnp.dot(
                weights.astype(jnp.bfloat16), kv_ref[1, :width], preferred_element_type=jnp.float32
            )
            peak[head, here, :] = top

    mine = order_ref[me]

    def seen(far):
        return (
            order_ref[ring_index(lax.rem(place + count - far, count), count)] < mine,
            order_ref[ring_index(lax.rem(place + far, count), count)] < mine,
        )

    def weigh(head, far, k_left, k_right):
        see_left, see_right = seen(far)
        q = q_ref[:, head * HD : (head + 1) * HD]
        first = dot_t(q, k_left)
        second = dot_t(q, k_right)
        old = peak[head]
        top_first = jnp.where(see_left, jnp.max(first, axis=1, keepdims=True), LOW)
        top_second = jnp.where(see_right, jnp.max(second, axis=1, keepdims=True), LOW)
        top = jnp.maximum(old, jnp.maximum(top_first, top_second))
        keep = jnp.exp2((old - top) * SCALE2)
        shift_first = jnp.where(see_left, top, -LOW)
        shift_second = jnp.where(see_right, top, -LOW)
        w_first = jnp.exp2((first - lanes(shift_first, k_left.shape[0])) * SCALE2)
        w_second = jnp.exp2((second - lanes(shift_second, k_right.shape[0])) * SCALE2)
        new_total = total[head] * keep + (lane_sum(w_first) + lane_sum(w_second))
        return top, keep, new_total, w_first.astype(jnp.bfloat16), w_second.astype(jnp.bfloat16)

    def advance(j, carry):
        for rightward in (True, False):
            remote(kv_ref.at[:, side(j, rightward)], landing(j, rightward), j, rightward).wait_recv()

        @pl.when(j + PARTS < steps - 1)
        def _():
            for rightward in (True, False):
                forward(j + PARTS, rightward).start()

        for i in range(tails):

            @pl.when(j + PARTS == steps + i)
            def _(i=i):
                for rightward in (True, False):
                    tail_copy(i, 0, rightward).start()
                if i == tails - 1:
                    for rightward in (True, False):
                        forward(steps - 1, rightward).start()
                    for late in range(tails):
                        for rightward in (True, False):
                            tail_copy(late, 1, rightward).start()

        block = lax.div(j, PARTS)
        on_left, on_right = side(j, True), side(j, False)
        for head in range(QH):
            top, keep, new_total, w_first, w_second = weigh(
                head, 1 + block, from_left[block, 0, on_left], from_right[block, 0, on_right]
            )
            total[head] = new_total
            acc[head] = acc[head] * keep + (
                jnp.dot(w_first, from_left[block, 1, on_left], preferred_element_type=jnp.float32)
                + jnp.dot(w_second, from_right[block, 1, on_right], preferred_element_type=jnp.float32)
            )
            peak[head] = top
        return carry

    lax.fori_loop(0, steps - 1, advance, 0)
    for i in range(tails):
        for rightward in (True, False):
            tail_copy(i, 0, rightward).wait_recv()
    on_left, on_right = tail_keys[:, 0].reshape(tails * piece, HD), tail_keys[:, 1].reshape(tails * piece, HD)
    for head in range(QH):
        top, keep, new_total, w_first, w_second = weigh(head, whole + 1, on_left, on_right)
        for i in range(tails):
            here = slice(i * piece, (i + 1) * piece)
            tail_weights[i, head, :, :piece] = w_first[:, here]
            tail_weights[i, head, :, piece:] = w_second[:, here]
        acc[head] = acc[head] * keep
        total[head] = new_total
        peak[head] = top

    for rightward in (True, False):
        forward(steps - 1, rightward).wait_recv()
    left_keys, left_values = landing(steps - 1, True).at[0], landing(steps - 1, True).at[1]
    right_keys, right_values = landing(steps - 1, False).at[0], landing(steps - 1, False).at[1]
    for head in range(QH):
        top, keep, new_total, w_first, w_second = weigh(head, whole, left_keys[...], right_keys[...])
        inverse = 1.0 / jnp.sum(new_total, axis=1, keepdims=True)
        acc[head] = (
            acc[head] * keep
            + jnp.dot(w_first, left_values[...], preferred_element_type=jnp.float32)
            + jnp.dot(w_second, right_values[...], preferred_element_type=jnp.float32)
        ) * inverse
        total[head] = keep * inverse
    for i in range(tails):
        for rightward in (True, False):
            tail_copy(i, 1, rightward).wait_recv()
        values = tail_values[i].reshape(2 * piece, HD)
        for head in range(QH):
            summed = acc[head] + total[head] * jnp.dot(
                tail_weights[i, head], values, preferred_element_type=jnp.float32
            )
            if i < tails - 1:
                acc[head] = summed
            else:
                out_ref[:, head * HD : (head + 1) * HD] = summed.astype(out_ref.dtype)

    def drain(j, carry):
        for rightward in (True, False):
            remote(kv_ref.at[:, side(j, rightward)], landing(j, rightward), j, rightward).wait_send()
        return carry

    lax.fori_loop(0, steps, drain, 0)
    for i in range(tails):
        for which in range(2):
            for rightward in (True, False):
                tail_copy(i, which, rightward).wait_send()


def solution(mesh):
    count = mesh.shape["ctx"]
    whole = count // 2 - 1
    sends = PARTS * whole + PARTS

    def body(queries, key_rows, value_rows, block_order):
        rows = queries.shape[0]
        slots = pltpu.VMEM((whole, 2, rows, HD), key_rows.dtype)
        piece, half = rows // PARTS, PARTS // 2
        tails = [
            pltpu.VMEM((half, 2, piece, HD), key_rows.dtype),
            pltpu.VMEM((half, 2, piece, HD), value_rows.dtype),
            pltpu.VMEM((half, QH, rows, 2 * piece), jnp.bfloat16),
        ]
        stats = pltpu.VMEM((QH, rows, HD), jnp.float32)
        sems = pltpu.SemaphoreType.DMA((sends,))
        local = [
            pltpu.SMEM(block_order.shape, block_order.dtype),
            pltpu.VMEM(queries.shape, queries.dtype),
            pltpu.VMEM((2, rows, HD), key_rows.dtype),
        ]
        return pl.pallas_call(
            functools.partial(kernel, count),
            out_shape=jax.ShapeDtypeStruct(queries.shape, queries.dtype),
            in_specs=[pl.BlockSpec(memory_space=pltpu.HBM)] * 4,
            out_specs=pl.BlockSpec(memory_space=pltpu.VMEM),
            scratch_shapes=local + [slots] * 2 + tails + [stats] * 3 + [sems] * 4 + [pltpu.SemaphoreType.DMA((4,))],
            compiler_params=pltpu.CompilerParams(
                collective_id=0, has_side_effects=True, vmem_limit_bytes=48 * 1024 * 1024
            ),
        )(*(pltpu.with_memory_space_constraint(x, pltpu.HBM) for x in (block_order, queries, key_rows, value_rows)))

    in_specs = (P("ctx", "head"), P("ctx", "head"), P("ctx", "head"), P())
    return jax.shard_map(body, mesh=mesh, in_specs=in_specs, out_specs=P("ctx", "head"), check_vma=False)
```

```python
import functools

import jax
import jax.numpy as jnp
from jax import lax
from jax.experimental import pallas as pl
from jax.experimental.pallas import tpu as pltpu
from jax.sharding import PartitionSpec as P

HD = 128
QH = 2
PARTS = 4
TILES = 4
SCALE2 = 168.0 ** (-0.5) * 1.4426950408889634
LOW = -1e30


def ring_place(index, count):
    side = lax.rem(index, 2)
    level = lax.div(index, 2)
    return level * (1 - side) + (count - 1 - level) * side


def ring_index(place, count):
    side = lax.div(place, count // 2)
    level = place * (1 - side) + (count - 1 - place) * side
    return level * 2 + side


def lanes(column, width):
    return jnp.concatenate([column] * (width // HD), axis=1)


def dot_t(a, b):
    return lax.dot_general(a, b, (((1,), (1,)), ((), ())), preferred_element_type=jnp.float32)


def lane_sum(weights):
    total = weights[:, :HD]
    for start in range(HD, weights.shape[1], HD):
        total = total + weights[:, start : start + HD]
    return total


def kernel(
    count, order_hbm, q_hbm, k_hbm, v_hbm, out_ref,
    order_ref, q_ref, kv_ref, from_left, from_right, tail_keys, tail_values, tail_weights, scales, acc, peak, total,
    to_right_sem, to_left_sem, from_left_sem, from_right_sem, loaded,
):
    me = lax.axis_index("ctx")
    rows = q_ref.shape[0]
    piece = rows // PARTS
    whole = count // 2 - 1
    steps = PARTS * whole
    tails = PARTS // 2
    place = ring_place(me, count)
    right = ring_index(lax.rem(place + 1, count), count)
    left = ring_index(lax.rem(place + count - 1, count), count)

    barrier = pltpu.get_barrier_semaphore()
    for neighbour in (left, right):
        pl.semaphore_signal(barrier, inc=1, device_id={"ctx": neighbour}, device_id_type=pl.DeviceIdType.MESH)
    moves = [(k_hbm, kv_ref.at[0]), (v_hbm, kv_ref.at[1]), (q_hbm, q_ref), (order_hbm, order_ref)]
    loads = [pltpu.make_async_copy(src, dst, loaded.at[i]) for i, (src, dst) in enumerate(moves)]
    for load in loads:
        load.start()
    for load in loads[:2]:
        load.wait()
    pl.semaphore_wait(barrier, 2)

    def remote(src, dst, j, rightward):
        send, recv, target = (to_right_sem, from_left_sem, right) if rightward else (to_left_sem, from_right_sem, left)
        return pltpu.make_async_remote_copy(
            src_ref=src, dst_ref=dst, send_sem=send.at[j], recv_sem=recv.at[j],
            device_id={"ctx": target}, device_id_type=pl.DeviceIdType.MESH,
        )

    def side(j, rightward):
        part = lax.rem(j + (0 if rightward else tails), PARTS)
        return pl.ds(pl.multiple_of(part * piece, piece), piece)

    def landing(j, rightward):
        return (from_left if rightward else from_right).at[lax.div(j, PARTS), :, side(j, rightward)]

    def forward(j, rightward):
        return remote(landing(j - PARTS, rightward), landing(j, rightward), j, rightward)

    def tail_copy(i, which, rightward):
        src, own = (from_left, 0) if rightward else (from_right, 1)
        dst = (tail_keys, tail_values)[which]
        block, part = (whole - 1, i - 1) if i else (whole - 2, PARTS - 1)
        return remote(
            src.at[block, which, side(part, rightward)], dst.at[i, own], steps - 1 + 2 * i + which, rightward
        )

    for j in range(PARTS):
        for rightward in (True, False):
            remote(kv_ref.at[:, side(j, rightward)], landing(j, rightward), j, rightward).start()
    for load in loads[2:]:
        load.wait()

    tile_rows = rows // TILES
    for head in range(QH):
        cols = slice(head * HD, (head + 1) * HD)
        for tile in range(TILES):
            here = slice(tile * tile_rows, (tile + 1) * tile_rows)
            width = (tile + 1) * tile_rows
            scores = dot_t(q_ref[here, cols], kv_ref[0, :width])
            row_ids = lax.broadcasted_iota(jnp.int32, (tile_rows, width), 0) + tile * tile_rows
            column_ids = lax.broadcasted_iota(jnp.int32, (tile_rows, width), 1)
            scores = jnp.where(column_ids <= row_ids, scores, LOW)
            top = jnp.broadcast_to(jnp.max(scores, axis=1, keepdims=True), (tile_rows, HD))
            weights = jnp.exp2((scores - lanes(top, width)) * SCALE2)
            total[head, here, :] = lane_sum(weights)
            acc[head, here, :] = jnp.dot(
                weights.astype(jnp.bfloat16), kv_ref[1, :width], preferred_element_type=jnp.float32
            )
            peak[head, here, :] = top

    mine = order_ref[me]

    def seen(far):
        return (
            order_ref[ring_index(lax.rem(place + count - far, count), count)] < mine,
            order_ref[ring_index(lax.rem(place + far, count), count)] < mine,
        )

    def weigh(head, far, k_left, k_right):
        see_left, see_right = seen(far)
        q = q_ref[:, head * HD : (head + 1) * HD]
        first = dot_t(q, k_left)
        second = dot_t(q, k_right)
        old = peak[head]
        top_first = jnp.where(see_left, jnp.max(first, axis=1, keepdims=True), LOW)
        top_second = jnp.where(see_right, jnp.max(second, axis=1, keepdims=True), LOW)
        top = jnp.maximum(old, jnp.maximum(top_first, top_second))
        keep = jnp.exp2((old - top) * SCALE2)
        shift_first = jnp.where(see_left, top, -LOW)
        shift_second = jnp.where(see_right, top, -LOW)
        w_first = jnp.exp2((first - lanes(shift_first, k_left.shape[0])) * SCALE2)
        w_second = jnp.exp2((second - lanes(shift_second, k_right.shape[0])) * SCALE2)
        new_total = total[head] * keep + (lane_sum(w_first) + lane_sum(w_second))
        return top, keep, new_total, w_first.astype(jnp.bfloat16), w_second.astype(jnp.bfloat16)

    def advance(j, carry):
        for rightward in (True, False):
            remote(kv_ref.at[:, side(j, rightward)], landing(j, rightward), j, rightward).wait_recv()

        @pl.when(j + PARTS < steps - 1)
        def _():
            for rightward in (True, False):
                forward(j + PARTS, rightward).start()

        for i in range(tails + 1):

            @pl.when(j + PARTS == steps - 1 + i)
            def _(i=i):
                wanted = [(i, 0)] + ([(late, 1) for late in range(tails + 1)] if i == tails else [])
                for at, which in wanted:
                    for rightward in (True, False):
                        tail_copy(at, which, rightward).start()

        block = lax.div(j, PARTS)
        on_left, on_right = side(j, True), side(j, False)
        for head in range(QH):
            top, keep, new_total, w_first, w_second = weigh(
                head, 1 + block, from_left[block, 0, on_left], from_right[block, 0, on_right]
            )
            total[head] = new_total
            acc[head] = acc[head] * keep + (
                jnp.dot(w_first, from_left[block, 1, on_left], preferred_element_type=jnp.float32)
                + jnp.dot(w_second, from_right[block, 1, on_right], preferred_element_type=jnp.float32)
            )
            peak[head] = top
        return carry

    lax.fori_loop(0, steps - 1, advance, 0)
    for i in range(tails + 1):
        for rightward in (True, False):
            tail_copy(i, 0, rightward).wait_recv()
        for head in range(QH):
            top, keep, new_total, w_first, w_second = weigh(
                head, whole + min(i, 1), tail_keys[i, 0], tail_keys[i, 1]
            )
            tail_weights[i, head, :, :piece] = w_first
            tail_weights[i, head, :, piece:] = w_second
            if i < tails:
                peak[head] = top
                total[head] = new_total
                change = keep
            else:
                inverse = jnp.broadcast_to(1.0 / jnp.sum(new_total, axis=1, keepdims=True), (rows, HD))
                scales[i, head] = inverse
                change = keep * inverse
            acc[head] = acc[head] * change
            for earlier in range(i):
                scales[earlier, head] = change if earlier == i - 1 else scales[earlier, head] * change
    for i in range(tails + 1):
        for rightward in (True, False):
            tail_copy(i, 1, rightward).wait_recv()
        values = tail_values[i].reshape(2 * piece, HD)
        for head in range(QH):
            summed = acc[head] + scales[i, head] * jnp.dot(
                tail_weights[i, head], values, preferred_element_type=jnp.float32
            )
            if i < tails:
                acc[head] = summed
            else:
                out_ref[:, head * HD : (head + 1) * HD] = summed.astype(out_ref.dtype)

    def drain(j, carry):
        for rightward in (True, False):
            remote(kv_ref.at[:, side(j, rightward)], landing(j, rightward), j, rightward).wait_send()
        return carry

    lax.fori_loop(0, steps - 1, drain, 0)
    for i in range(tails + 1):
        for which in range(2):
            for rightward in (True, False):
                tail_copy(i, which, rightward).wait_send()


def solution(mesh):
    count = mesh.shape["ctx"]
    whole = count // 2 - 1
    sends = PARTS * whole + 1 + 2 * (PARTS // 2)

    def body(queries, key_rows, value_rows, block_order):
        rows = queries.shape[0]
        slots = pltpu.VMEM((whole, 2, rows, HD), key_rows.dtype)
        piece, late = rows // PARTS, PARTS // 2 + 1
        tails = [
            pltpu.VMEM((late, 2, piece, HD), key_rows.dtype),
            pltpu.VMEM((late, 2, piece, HD), value_rows.dtype),
            pltpu.VMEM((late, QH, rows, 2 * piece), jnp.bfloat16),
            pltpu.VMEM((late, QH, rows, HD), jnp.float32),
        ]
        stats = pltpu.VMEM((QH, rows, HD), jnp.float32)
        sems = pltpu.SemaphoreType.DMA((sends,))
        local = [
            pltpu.SMEM(block_order.shape, block_order.dtype),
            pltpu.VMEM(queries.shape, queries.dtype),
            pltpu.VMEM((2, rows, HD), key_rows.dtype),
        ]
        return pl.pallas_call(
            functools.partial(kernel, count),
            out_shape=jax.ShapeDtypeStruct(queries.shape, queries.dtype),
            in_specs=[pl.BlockSpec(memory_space=pltpu.HBM)] * 4,
            out_specs=pl.BlockSpec(memory_space=pltpu.VMEM),
            scratch_shapes=local + [slots] * 2 + tails + [stats] * 3 + [sems] * 4 + [pltpu.SemaphoreType.DMA((4,))],
            compiler_params=pltpu.CompilerParams(
                collective_id=0, has_side_effects=True, vmem_limit_bytes=48 * 1024 * 1024
            ),
        )(*(pltpu.with_memory_space_constraint(x, pltpu.HBM) for x in (block_order, queries, key_rows, value_rows)))

    in_specs = (P("ctx", "head"), P("ctx", "head"), P("ctx", "head"), P())
    return jax.shard_map(body, mesh=mesh, in_specs=in_specs, out_specs=P("ctx", "head"), check_vma=False)
```

```python
import functools

import jax
import jax.numpy as jnp
from jax import lax
from jax.experimental import pallas as pl
from jax.experimental.pallas import tpu as pltpu
from jax.sharding import PartitionSpec as P

HD = 128
QH = 2
PARTS = 4
EARLY = 2
TILES = 4
SCALE2 = 168.0 ** (-0.5) * 1.4426950408889634
LOW = -1e30


def ring_place(index, count):
    side = lax.rem(index, 2)
    level = lax.div(index, 2)
    return level * (1 - side) + (count - 1 - level) * side


def ring_index(place, count):
    side = lax.div(place, count // 2)
    level = place * (1 - side) + (count - 1 - place) * side
    return level * 2 + side


def lanes(column, width):
    return jnp.concatenate([column] * (width // HD), axis=1)


def dot_t(a, b):
    return lax.dot_general(a, b, (((1,), (1,)), ((), ())), preferred_element_type=jnp.float32)


def lane_sum(weights):
    total = weights[:, :HD]
    for start in range(HD, weights.shape[1], HD):
        total = total + weights[:, start : start + HD]
    return total


def kernel(
    count, order_hbm, q_hbm, k_hbm, v_hbm, out_ref,
    order_ref, q_ref, kv_ref, from_left, from_right, tail_keys, tail_values, tail_weights, scales, acc, peak, total,
    to_right_sem, to_left_sem, from_left_sem, from_right_sem, loaded,
):
    me = lax.axis_index("ctx")
    rows = q_ref.shape[0]
    piece = rows // PARTS
    whole = count // 2 - 1
    steps = PARTS * whole
    half = PARTS // 2
    tails = EARLY + half - 1
    place = ring_place(me, count)
    right = ring_index(lax.rem(place + 1, count), count)
    left = ring_index(lax.rem(place + count - 1, count), count)

    barrier = pltpu.get_barrier_semaphore()
    for neighbour in (left, right):
        pl.semaphore_signal(barrier, inc=1, device_id={"ctx": neighbour}, device_id_type=pl.DeviceIdType.MESH)
    moves = [(k_hbm, kv_ref.at[0]), (v_hbm, kv_ref.at[1]), (q_hbm, q_ref), (order_hbm, order_ref)]
    loads = [pltpu.make_async_copy(src, dst, loaded.at[i]) for i, (src, dst) in enumerate(moves)]
    for load in loads:
        load.start()
    for load in loads[:2]:
        load.wait()
    pl.semaphore_wait(barrier, 2)

    def remote(src, dst, j, rightward):
        send, recv, target = (to_right_sem, from_left_sem, right) if rightward else (to_left_sem, from_right_sem, left)
        return pltpu.make_async_remote_copy(
            src_ref=src, dst_ref=dst, send_sem=send.at[j], recv_sem=recv.at[j],
            device_id={"ctx": target}, device_id_type=pl.DeviceIdType.MESH,
        )

    def side(j, rightward):
        part = lax.rem(j + (0 if rightward else half), PARTS)
        return pl.ds(pl.multiple_of(part * piece, piece), piece)

    def landing(j, rightward):
        return (from_left if rightward else from_right).at[lax.div(j, PARTS), :, side(j, rightward)]

    def forward(j, rightward):
        return remote(landing(j - PARTS, rightward), landing(j, rightward), j, rightward)

    def tail_copy(i, which, rightward):
        src, own = (from_left, 0) if rightward else (from_right, 1)
        dst = (tail_keys, tail_values)[which]
        block, part = (whole - 1, i - EARLY) if i >= EARLY else (whole - 2, PARTS - EARLY + i)
        return remote(
            src.at[block, which, side(part, rightward)], dst.at[i, own], steps - EARLY + 2 * i + which, rightward
        )

    for j in range(PARTS):
        for rightward in (True, False):
            remote(kv_ref.at[:, side(j, rightward)], landing(j, rightward), j, rightward).start()
    for load in loads[2:]:
        load.wait()

    tile_rows = rows // TILES
    for head in range(QH):
        cols = slice(head * HD, (head + 1) * HD)
        for tile in range(TILES):
            here = slice(tile * tile_rows, (tile + 1) * tile_rows)
            width = (tile + 1) * tile_rows
            scores = dot_t(q_ref[here, cols], kv_ref[0, :width])
            row_ids = lax.broadcasted_iota(jnp.int32, (tile_rows, width), 0) + tile * tile_rows
            column_ids = lax.broadcasted_iota(jnp.int32, (tile_rows, width), 1)
            scores = jnp.where(column_ids <= row_ids, scores, LOW)
            top = jnp.broadcast_to(jnp.max(scores, axis=1, keepdims=True), (tile_rows, HD))
            weights = jnp.exp2((scores - lanes(top, width)) * SCALE2)
            total[head, here, :] = lane_sum(weights)
            acc[head, here, :] = jnp.dot(
                weights.astype(jnp.bfloat16), kv_ref[1, :width], preferred_element_type=jnp.float32
            )
            peak[head, here, :] = top

    mine = order_ref[me]

    def seen(far):
        return (
            order_ref[ring_index(lax.rem(place + count - far, count), count)] < mine,
            order_ref[ring_index(lax.rem(place + far, count), count)] < mine,
        )

    def weigh(head, far, k_left, k_right):
        see_left, see_right = seen(far)
        q = q_ref[:, head * HD : (head + 1) * HD]
        first = dot_t(q, k_left)
        second = dot_t(q, k_right)
        old = peak[head]
        top_first = jnp.where(see_left, jnp.max(first, axis=1, keepdims=True), LOW)
        top_second = jnp.where(see_right, jnp.max(second, axis=1, keepdims=True), LOW)
        top = jnp.maximum(old, jnp.maximum(top_first, top_second))
        keep = jnp.exp2((old - top) * SCALE2)
        shift_first = jnp.where(see_left, top, -LOW)
        shift_second = jnp.where(see_right, top, -LOW)
        w_first = jnp.exp2((first - lanes(shift_first, k_left.shape[0])) * SCALE2)
        w_second = jnp.exp2((second - lanes(shift_second, k_right.shape[0])) * SCALE2)
        new_total = total[head] * keep + (lane_sum(w_first) + lane_sum(w_second))
        return top, keep, new_total, w_first.astype(jnp.bfloat16), w_second.astype(jnp.bfloat16)

    def advance(j, carry):
        for rightward in (True, False):
            remote(kv_ref.at[:, side(j, rightward)], landing(j, rightward), j, rightward).wait_recv()

        @pl.when(j + PARTS < steps - EARLY)
        def _():
            for rightward in (True, False):
                forward(j + PARTS, rightward).start()

        for i in range(tails + 1):

            @pl.when(j + PARTS == steps - EARLY + i)
            def _(i=i):
                wanted = [(i, 0)] + ([(late, 1) for late in range(tails + 1)] if i == tails else [])
                for at, which in wanted:
                    for rightward in (True, False):
                        tail_copy(at, which, rightward).start()

        block = lax.div(j, PARTS)
        on_left, on_right = side(j, True), side(j, False)
        for head in range(QH):
            top, keep, new_total, w_first, w_second = weigh(
                head, 1 + block, from_left[block, 0, on_left], from_right[block, 0, on_right]
            )
            total[head] = new_total
            acc[head] = acc[head] * keep + (
                jnp.dot(w_first, from_left[block, 1, on_left], preferred_element_type=jnp.float32)
                + jnp.dot(w_second, from_right[block, 1, on_right], preferred_element_type=jnp.float32)
            )
            peak[head] = top
        return carry

    lax.fori_loop(0, steps - EARLY, advance, 0)
    for i in range(tails + 1):
        for rightward in (True, False):
            tail_copy(i, 0, rightward).wait_recv()
        for head in range(QH):
            top, keep, new_total, w_first, w_second = weigh(
                head, whole + (i >= EARLY), tail_keys[i, 0], tail_keys[i, 1]
            )
            tail_weights[i, head, :, :piece] = w_first
            tail_weights[i, head, :, piece:] = w_second
            if i < tails:
                peak[head] = top
                total[head] = new_total
                change = keep
            else:
                inverse = jnp.broadcast_to(1.0 / jnp.sum(new_total, axis=1, keepdims=True), (rows, HD))
                scales[i, head] = inverse
                change = keep * inverse
            acc[head] = acc[head] * change
            for earlier in range(i):
                scales[earlier, head] = change if earlier == i - 1 else scales[earlier, head] * change
    def drain(j, carry):
        for rightward in (True, False):
            remote(kv_ref.at[:, side(j, rightward)], landing(j, rightward), j, rightward).wait_send()
        return carry

    for i in range(tails + 1):
        if i == tails:
            lax.fori_loop(0, steps - EARLY, drain, 0)
            for rightward in (True, False):
                for sent in range(tails + 1):
                    tail_copy(sent, 0, rightward).wait_send()
                for sent in range(tails - 1):
                    tail_copy(sent, 1, rightward).wait_send()
        for rightward in (True, False):
            tail_copy(i, 1, rightward).wait_recv()
        values = tail_values[i].reshape(2 * piece, HD)
        for head in range(QH):
            summed = acc[head] + scales[i, head] * jnp.dot(
                tail_weights[i, head], values, preferred_element_type=jnp.float32
            )
            if i < tails:
                acc[head] = summed
            else:
                out_ref[:, head * HD : (head + 1) * HD] = summed.astype(out_ref.dtype)

    for i in (tails - 1, tails):
        for rightward in (True, False):
            tail_copy(i, 1, rightward).wait_send()


def solution(mesh):
    count = mesh.shape["ctx"]
    whole = count // 2 - 1
    late = EARLY + PARTS // 2
    sends = PARTS * whole - EARLY + 2 * late

    def body(queries, key_rows, value_rows, block_order):
        rows = queries.shape[0]
        slots = pltpu.VMEM((whole, 2, rows, HD), key_rows.dtype)
        piece = rows // PARTS
        tails = [
            pltpu.VMEM((late, 2, piece, HD), key_rows.dtype),
            pltpu.VMEM((late, 2, piece, HD), value_rows.dtype),
            pltpu.VMEM((late, QH, rows, 2 * piece), jnp.bfloat16),
            pltpu.VMEM((late, QH, rows, HD), jnp.float32),
        ]
        stats = pltpu.VMEM((QH, rows, HD), jnp.float32)
        sems = pltpu.SemaphoreType.DMA((sends,))
        local = [
            pltpu.SMEM(block_order.shape, block_order.dtype),
            pltpu.VMEM(queries.shape, queries.dtype),
            pltpu.VMEM((2, rows, HD), key_rows.dtype),
        ]
        return pl.pallas_call(
            functools.partial(kernel, count),
            out_shape=jax.ShapeDtypeStruct(queries.shape, queries.dtype),
            in_specs=[pl.BlockSpec(memory_space=pltpu.HBM)] * 4,
            out_specs=pl.BlockSpec(memory_space=pltpu.VMEM),
            scratch_shapes=local + [slots] * 2 + tails + [stats] * 3 + [sems] * 4 + [pltpu.SemaphoreType.DMA((4,))],
            compiler_params=pltpu.CompilerParams(
                collective_id=0, has_side_effects=True, vmem_limit_bytes=48 * 1024 * 1024
            ),
        )(*(pltpu.with_memory_space_constraint(x, pltpu.HBM) for x in (block_order, queries, key_rows, value_rows)))

    in_specs = (P("ctx", "head"), P("ctx", "head"), P("ctx", "head"), P())
    return jax.shard_map(body, mesh=mesh, in_specs=in_specs, out_specs=P("ctx", "head"), check_vma=False)
```

```python
import functools

import jax
import jax.numpy as jnp
from jax import lax
from jax.experimental import pallas as pl
from jax.experimental.pallas import tpu as pltpu
from jax.sharding import PartitionSpec as P

HD = 128
QH = 2
PARTS = 4
EARLY = 2
BANDS = 2
TILES = 4
SCALE2 = 168.0 ** (-0.5) * 1.4426950408889634
LOW = -1e30


def ring_place(index, count):
    side = lax.rem(index, 2)
    level = lax.div(index, 2)
    return level * (1 - side) + (count - 1 - level) * side


def ring_index(place, count):
    side = lax.div(place, count // 2)
    level = place * (1 - side) + (count - 1 - place) * side
    return level * 2 + side


def lanes(column, width):
    return jnp.concatenate([column] * (width // HD), axis=1)


def dot_t(a, b):
    return lax.dot_general(a, b, (((1,), (1,)), ((), ())), preferred_element_type=jnp.float32)


def lane_sum(weights):
    total = weights[:, :HD]
    for start in range(HD, weights.shape[1], HD):
        total = total + weights[:, start : start + HD]
    return total


def kernel(
    count, order_hbm, q_hbm, k_hbm, v_hbm, out_ref,
    order_ref, q_ref, kv_ref, from_left, from_right, tail_keys, tail_values, tail_weights, scales, acc, peak, total,
    to_right_sem, to_left_sem, from_left_sem, from_right_sem, loaded,
):
    me = lax.axis_index("ctx")
    rows = q_ref.shape[0]
    piece = rows // PARTS
    whole = count // 2 - 1
    steps = PARTS * whole
    half = PARTS // 2
    tails = EARLY + half - 1
    place = ring_place(me, count)
    right = ring_index(lax.rem(place + 1, count), count)
    left = ring_index(lax.rem(place + count - 1, count), count)

    barrier = pltpu.get_barrier_semaphore()
    for neighbour in (left, right):
        pl.semaphore_signal(barrier, inc=1, device_id={"ctx": neighbour}, device_id_type=pl.DeviceIdType.MESH)
    moves = [(k_hbm, kv_ref.at[0]), (v_hbm, kv_ref.at[1]), (q_hbm, q_ref), (order_hbm, order_ref)]
    loads = [pltpu.make_async_copy(src, dst, loaded.at[i]) for i, (src, dst) in enumerate(moves)]
    for load in loads:
        load.start()
    for load in loads[:2]:
        load.wait()
    pl.semaphore_wait(barrier, 2)

    def remote(src, dst, j, rightward):
        send, recv, target = (to_right_sem, from_left_sem, right) if rightward else (to_left_sem, from_right_sem, left)
        return pltpu.make_async_remote_copy(
            src_ref=src, dst_ref=dst, send_sem=send.at[j], recv_sem=recv.at[j],
            device_id={"ctx": target}, device_id_type=pl.DeviceIdType.MESH,
        )

    def side(j, rightward):
        part = lax.rem(j + (0 if rightward else half), PARTS)
        return pl.ds(pl.multiple_of(part * piece, piece), piece)

    def landing(j, rightward):
        return (from_left if rightward else from_right).at[lax.div(j, PARTS), :, side(j, rightward)]

    def forward(j, rightward):
        return remote(landing(j - PARTS, rightward), landing(j, rightward), j, rightward)

    def tail_copy(i, which, rightward):
        src, own = (from_left, 0) if rightward else (from_right, 1)
        dst = (tail_keys, tail_values)[which]
        block, part = (whole - 1, i - EARLY) if i >= EARLY else (whole - 2, PARTS - EARLY + i)
        return remote(
            src.at[block, which, side(part, rightward)], dst.at[i, own], steps - EARLY + 2 * i + which, rightward
        )

    for j in range(PARTS):
        for rightward in (True, False):
            remote(kv_ref.at[:, side(j, rightward)], landing(j, rightward), j, rightward).start()
    for load in loads[2:]:
        load.wait()

    tile_rows = rows // TILES
    for head in range(QH):
        cols = slice(head * HD, (head + 1) * HD)
        for tile in range(TILES):
            here = slice(tile * tile_rows, (tile + 1) * tile_rows)
            width = (tile + 1) * tile_rows
            scores = dot_t(q_ref[here, cols], kv_ref[0, :width])
            row_ids = lax.broadcasted_iota(jnp.int32, (tile_rows, width), 0) + tile * tile_rows
            column_ids = lax.broadcasted_iota(jnp.int32, (tile_rows, width), 1)
            scores = jnp.where(column_ids <= row_ids, scores, LOW)
            top = jnp.broadcast_to(jnp.max(scores, axis=1, keepdims=True), (tile_rows, HD))
            weights = jnp.exp2((scores - lanes(top, width)) * SCALE2)
            total[head, here, :] = lane_sum(weights)
            acc[head, here, :] = jnp.dot(
                weights.astype(jnp.bfloat16), kv_ref[1, :width], preferred_element_type=jnp.float32
            )
            peak[head, here, :] = top

    mine = order_ref[me]

    def seen(far):
        return (
            order_ref[ring_index(lax.rem(place + count - far, count), count)] < mine,
            order_ref[ring_index(lax.rem(place + far, count), count)] < mine,
        )

    def weigh(head, far, k_left, k_right):
        see_left, see_right = seen(far)
        q = q_ref[:, head * HD : (head + 1) * HD]
        first = dot_t(q, k_left)
        second = dot_t(q, k_right)
        old = peak[head]
        top_first = jnp.where(see_left, jnp.max(first, axis=1, keepdims=True), LOW)
        top_second = jnp.where(see_right, jnp.max(second, axis=1, keepdims=True), LOW)
        top = jnp.maximum(old, jnp.maximum(top_first, top_second))
        keep = jnp.exp2((old - top) * SCALE2)
        shift_first = jnp.where(see_left, top, -LOW)
        shift_second = jnp.where(see_right, top, -LOW)
        w_first = jnp.exp2((first - lanes(shift_first, k_left.shape[0])) * SCALE2)
        w_second = jnp.exp2((second - lanes(shift_second, k_right.shape[0])) * SCALE2)
        new_total = total[head] * keep + (lane_sum(w_first) + lane_sum(w_second))
        return top, keep, new_total, w_first.astype(jnp.bfloat16), w_second.astype(jnp.bfloat16)

    def advance(j, carry):
        for rightward in (True, False):
            remote(kv_ref.at[:, side(j, rightward)], landing(j, rightward), j, rightward).wait_recv()

        @pl.when(j + PARTS < steps - EARLY)
        def _():
            for rightward in (True, False):
                forward(j + PARTS, rightward).start()

        for i in range(tails + 1):

            @pl.when(j + PARTS == steps - EARLY + i)
            def _(i=i):
                wanted = [(i, 0)] + ([(late, 1) for late in range(tails + 1)] if i == tails else [])
                for at, which in wanted:
                    for rightward in (True, False):
                        tail_copy(at, which, rightward).start()

        block = lax.div(j, PARTS)
        on_left, on_right = side(j, True), side(j, False)
        for head in range(QH):
            top, keep, new_total, w_first, w_second = weigh(
                head, 1 + block, from_left[block, 0, on_left], from_right[block, 0, on_right]
            )
            total[head] = new_total
            acc[head] = acc[head] * keep + (
                jnp.dot(w_first, from_left[block, 1, on_left], preferred_element_type=jnp.float32)
                + jnp.dot(w_second, from_right[block, 1, on_right], preferred_element_type=jnp.float32)
            )
            peak[head] = top
        return carry

    lax.fori_loop(0, steps - EARLY, advance, 0)
    for i in range(tails + 1):
        for rightward in (True, False):
            tail_copy(i, 0, rightward).wait_recv()
        for head in range(QH):
            top, keep, new_total, w_first, w_second = weigh(
                head, whole + (i >= EARLY), tail_keys[i, 0], tail_keys[i, 1]
            )
            tail_weights[i, head, :, :piece] = w_first
            tail_weights[i, head, :, piece:] = w_second
            if i < tails:
                peak[head] = top
                total[head] = new_total
                change = keep
            else:
                inverse = jnp.broadcast_to(1.0 / jnp.sum(new_total, axis=1, keepdims=True), (rows, HD))
                scales[i, head] = inverse
                change = keep * inverse
            acc[head] = acc[head] * change
            for earlier in range(i):
                scales[earlier, head] = change if earlier == i - 1 else scales[earlier, head] * change
    def drain(j, carry):
        for rightward in (True, False):
            remote(kv_ref.at[:, side(j, rightward)], landing(j, rightward), j, rightward).wait_send()
        return carry

    for i in range(tails + 1):
        if i == tails:
            lax.fori_loop(0, steps - EARLY, drain, 0)
            for rightward in (True, False):
                for sent in range(tails + 1):
                    tail_copy(sent, 0, rightward).wait_send()
                for sent in range(tails - 1):
                    tail_copy(sent, 1, rightward).wait_send()
        for rightward in (True, False):
            tail_copy(i, 1, rightward).wait_recv()
        values = tail_values[i].reshape(2 * piece, HD)
        for head in range(QH):
            for start in range(0, rows, rows // BANDS):
                here = slice(start, start + rows // BANDS)
                summed = acc[head, here] + scales[i, head, here] * jnp.dot(
                    tail_weights[i, head, here], values, preferred_element_type=jnp.float32
                )
                if i < tails:
                    acc[head, here] = summed
                else:
                    out_ref[here, head * HD : (head + 1) * HD] = summed.astype(out_ref.dtype)

    for i in (tails - 1, tails):
        for rightward in (True, False):
            tail_copy(i, 1, rightward).wait_send()


def solution(mesh):
    count = mesh.shape["ctx"]
    whole = count // 2 - 1
    late = EARLY + PARTS // 2
    sends = PARTS * whole - EARLY + 2 * late

    def body(queries, key_rows, value_rows, block_order):
        rows = queries.shape[0]
        slots = pltpu.VMEM((whole, 2, rows, HD), key_rows.dtype)
        piece = rows // PARTS
        tails = [
            pltpu.VMEM((late, 2, piece, HD), key_rows.dtype),
            pltpu.VMEM((late, 2, piece, HD), value_rows.dtype),
            pltpu.VMEM((late, QH, rows, 2 * piece), jnp.bfloat16),
            pltpu.VMEM((late, QH, rows, HD), jnp.float32),
        ]
        stats = pltpu.VMEM((QH, rows, HD), jnp.float32)
        sems = pltpu.SemaphoreType.DMA((sends,))
        local = [
            pltpu.SMEM(block_order.shape, block_order.dtype),
            pltpu.VMEM(queries.shape, queries.dtype),
            pltpu.VMEM((2, rows, HD), key_rows.dtype),
        ]
        return pl.pallas_call(
            functools.partial(kernel, count),
            out_shape=jax.ShapeDtypeStruct(queries.shape, queries.dtype),
            in_specs=[pl.BlockSpec(memory_space=pltpu.HBM)] * 4,
            out_specs=pl.BlockSpec(memory_space=pltpu.VMEM),
            scratch_shapes=local + [slots] * 2 + tails + [stats] * 3 + [sems] * 4 + [pltpu.SemaphoreType.DMA((4,))],
            compiler_params=pltpu.CompilerParams(
                collective_id=0, has_side_effects=True, vmem_limit_bytes=48 * 1024 * 1024
            ),
        )(*(pltpu.with_memory_space_constraint(x, pltpu.HBM) for x in (block_order, queries, key_rows, value_rows)))

    in_specs = (P("ctx", "head"), P("ctx", "head"), P("ctx", "head"), P())
    return jax.shard_map(body, mesh=mesh, in_specs=in_specs, out_specs=P("ctx", "head"), check_vma=False)
```
